32 devices in a mesh: member: 2 (over y), polar: 4 (over z), azimuth: 4 (over x, core).
Axes of the slice: x: 2, y: 2, z: 4, core: 2. Of those that a mesh axis runs over, the one named last changes fastest.
Arguments:
- conv_out: bfloat16 [32, 720, 640], P(('member', 'polar'), 'azimuth'), parts along dimension 0, may hold values from -6 to 6
- grad_out: bfloat16 [32, 720, 640], P(('member', 'polar'), 'azimuth'), parts along dimension 0, may hold values from -6 to 6
- w_in: bfloat16 [640, 1280], replicated, may hold values from -0.25 to 0.25
- b_in: float32 [1280], replicated, may hold values from -4 to 4
- w_out: bfloat16 [1280, 640], replicated, may hold values from -0.15625 to 0.15625
- basis_weight: float32 [9, 640], replicated, may hold values from -1 to 1
- filt: bfloat16 [9, 16, 640], replicated, may hold values from -2 to 2
- offsets: int32 [16, 9], replicated, may hold values from 0 to 15, as said below
Outputs:
- grad_in: bfloat16 [32, 720, 640], P(('member', 'polar'), 'azimuth'), parts along dimension 0
The draws below stay inside these ranges and needn't reach their ends.
There are 2 independent parts, one for each index of `member`. The reference program is written for one: setup_inputs(seed, part) draws one part's arguments, and reference() takes and returns one part's arrays. A program takes and returns all parts, laid end to end along the dimension named above; an argument that names none is the same for every part. Nothing has to cross between parts.
Inputs may be any that keep to these rules, and one draw needn't show every extreme that they name: offsets[i, k] lies within 3 rows of i; column 0 is i, column 1 is min(i + 3, 15), column 2 is max(i - 3, 0).
All inputs are finite; a program needn't handle non-finite values.
Results may differ from the reference program's by a relative error of at most 0.006.
Values may be sent and summed in bfloat16 or wider, within the bound.
A program may use at most 64 MiB of HBM per device.

```python
import math
import jax
import jax.numpy as jnp
from jax import lax

CHANNELS = 640
HIDDEN_SIZE = 1280
NLON = 720
MODES = 320
BASES = 9
REACH = 3
NLAT = 16


def draw_offsets(key, part):
    rows = jnp.arange(NLAT, dtype=jnp.int32)[:, None]
    column = jnp.arange(BASES, dtype=jnp.int32)[None, :]
    drawn = jax.random.randint(jax.random.fold_in(key, 17), (NLAT, BASES), -REACH, REACH + 1, dtype=jnp.int32)
    shift_rows = jnp.where(column == 0, 0, jnp.where(column == 1, REACH, jnp.where(column == 2, -REACH, drawn)))
    return jnp.clip(rows + shift_rows, 0, NLAT - 1).astype(jnp.int32)


def shard_levels(stream_key, shape, shards, low, largest):
    gain = 1.0
    for axis_at, blocks in shards:
        draws = jax.random.uniform(jax.random.fold_in(jax.random.fold_in(stream_key, 6), axis_at), (blocks,), jnp.float32, low / len(shards), largest / len(shards))
        gain = gain * jnp.repeat(jnp.exp(draws), shape[axis_at] // blocks).reshape((-1,) + (1,) * (len(shape) - 1 - axis_at))
    return gain


def normal_values(key, dims, scale, limit, pieces=(), held_as=jnp.bfloat16):
    values = scale * jax.random.normal(key, dims, jnp.float32)
    if pieces:
        values = values * shard_levels(key, dims, pieces, -0.22, 0.18)
    return jnp.clip(values, -limit, limit).astype(held_as)


def setup_inputs(seed: int = 0, part: int = 0) -> dict:
    key_list = jax.random.split(jax.random.key(seed), 9)
    part_keys = jax.random.split(jax.random.fold_in(key_list[8], part), 9)
    conv_out = normal_values(part_keys[0], (NLAT, NLON, CHANNELS), 1.0, 6.0, ((0, 4), (1, 4)))
    grad_out = normal_values(part_keys[1], (NLAT, NLON, CHANNELS), 1.0, 6.0, ((0, 4), (1, 4)))
    w_in = normal_values(key_list[2], (CHANNELS, HIDDEN_SIZE), CHANNELS ** -0.5, 0.25)
    b_in = normal_values(key_list[3], (HIDDEN_SIZE,), 1.0, 4.0, (), jnp.float32)
    w_out = normal_values(key_list[4], (HIDDEN_SIZE, CHANNELS), HIDDEN_SIZE ** -0.5, 0.15625)
    basis_weight = jnp.clip(jax.random.uniform(key_list[5], (BASES, CHANNELS), jnp.float32, -1.0, 1.0), -1.0, 1.0)
    filt = normal_values(key_list[6], (BASES, NLAT, 2 * MODES), 0.33, 2.0)
    offsets = draw_offsets(jax.random.fold_in(key_list[8], 71), part)
    return {"conv_out": conv_out, "grad_out": grad_out, "w_in": w_in, "b_in": b_in, "w_out": w_out, "basis_weight": basis_weight, "filt": filt, "offsets": offsets}


def gelu_slope(values):
    normal_cdf = 0.5 * (1.0 + jax.scipy.special.erf(values / math.sqrt(2.0)))
    density = jnp.exp(-0.5 * values * values) / math.sqrt(2.0 * math.pi)
    return normal_cdf + values * density

def fourier_tables(length, modes):
    positions = jnp.arange(length, dtype=jnp.int32)
    waves = jnp.arange(modes, dtype=jnp.int32)
    phase = positions[:, None] * waves[None, :] % length
    angle = 2.0 * math.pi / length * phase.astype(jnp.float32)
    scale = 1.0 / math.sqrt(length)
    factor = jnp.where(waves == 0, 1.0, 2.0).astype(jnp.float32)
    analysis = (jnp.concatenate([jnp.cos(angle), -jnp.sin(angle)], axis=1) * scale).astype(jnp.bfloat16)
    synth = jnp.concatenate([jnp.cos(angle) * factor[None, :], -jnp.sin(angle) * factor[None, :]], axis=1) * scale
    return (analysis, jnp.transpose(synth).astype(jnp.bfloat16))

def spectral_term(spectrum, psi, weight):
    half = psi.shape[-1] // 2
    psi_full = psi.astype(jnp.float32)
    psi_real = psi_full[:, None, :half]
    psi_imag = psi_full[:, None, half:]
    spec_real = spectrum[:, :, :half]
    spec_imag = spectrum[:, :, half:]
    real_part = psi_real * spec_real + psi_imag * spec_imag
    imag_part = psi_real * spec_imag - psi_imag * spec_real
    return jnp.concatenate([real_part, imag_part], axis=2) * weight[None, :, None]

def reference(conv_out, grad_out, w_in, b_in, w_out, basis_weight, filt, offsets):

    def mlp_row(pair):
        h_row, g_row = pair
        pre = jnp.dot(h_row, w_in, preferred_element_type=jnp.float32) + b_in[None, :]
        back = lax.dot_general(g_row, w_out, (((1,), (1,)), ((), ())), preferred_element_type=jnp.float32)
        slope_grad = (back * gelu_slope(pre)).astype(jnp.bfloat16)
        hidden = lax.dot_general(slope_grad, w_in, (((1,), (1,)), ((), ())), preferred_element_type=jnp.float32)
        return hidden.astype(jnp.bfloat16)
    hidden_grad = lax.map(mlp_row, (conv_out, grad_out))
    hidden_grad = lax.optimization_barrier(hidden_grad)
    analysis, synthesis = fourier_tables(NLON, MODES)
    spectrum = jnp.einsum('inc,nm->icm', hidden_grad.astype(jnp.float32), analysis.astype(jnp.float32), precision=lax.Precision.HIGHEST)
    outspec = jnp.zeros(spectrum.shape, jnp.float32)
    for basis in range(BASES):
        contrib = spectral_term(spectrum, filt[basis], basis_weight[basis])
        outspec = outspec.at[offsets[:, basis]].add(contrib)
    rounded = lax.optimization_barrier(outspec.astype(jnp.bfloat16))
    conv_grad = jnp.einsum('jcm,mn->jnc', rounded.astype(jnp.float32), synthesis.astype(jnp.float32), precision=lax.Precision.HIGHEST).astype(jnp.bfloat16)
    return (grad_out.astype(jnp.float32) + conv_grad.astype(jnp.float32)).astype(jnp.bfloat16)
```

```python
import functools
import math

import jax
import jax.numpy as jnp
import ml_dtypes
import numpy as np
from jax import lax
from jax.experimental import pallas as pl
from jax.experimental.pallas import tpu as pltpu
from jax.sharding import PartitionSpec as P

REACH = 3
LANES = 128
MESH = pl.DeviceIdType.MESH
F32 = jnp.float32
BF16 = jnp.bfloat16


def fourier_tables(length, modes):
    phase = np.arange(length)[:, None] * np.arange(modes)[None, :] % length
    angle = 2.0 * math.pi / length * phase
    scale = 1.0 / math.sqrt(length)
    factor = np.where(np.arange(modes) == 0, 1.0, 2.0)[None, :]
    analysis = np.concatenate([np.cos(angle), -np.sin(angle)], axis=1) * scale
    synth = np.concatenate([np.cos(angle) * factor, -np.sin(angle) * factor], axis=1) * scale
    return analysis, synth


def gelu_slope(values):
    normal_cdf = 0.5 * (1.0 + lax.erf(values * (1.0 / math.sqrt(2.0))))
    density = jnp.exp(-0.5 * values * values) * (1.0 / math.sqrt(2.0 * math.pi))
    return normal_cdf + values * density


def dot(a, b):
    return jnp.dot(a, b, preferred_element_type=F32)


def dot_nt(a, b):
    return lax.dot_general(a, b, (((1,), (1,)), ((), ())), preferred_element_type=F32)


def dot_tn(a, b):
    return lax.dot_general(a, b, (((0,), (0,)), ((), ())), preferred_element_type=F32)


def kernel(
    parts, bands, conv, grad, w_in, b_in, w_out, wexp, target, fsel, ana, syn,
    out,
    w_perm, slope, tails, send, recv, spec, spec_tail, gain, outspec, ret_send, ret_recv,
    a_send, a_recv, z_send, z_recv, r_send, r_recv,
):
    rows, lon, channels = conv.shape
    hidden = w_in.shape[1]
    chan_part = channels // parts
    tail = chan_part - LANES
    me = lax.axis_index("azimuth")
    band = lax.axis_index("polar")
    bases2 = wexp.shape[0]
    width = rows + 2 * REACH
    modes2 = ana.shape[1]
    modes = modes2 // 2
    has_low = band > 0
    has_high = band < bands - 1

    barrier = pltpu.get_barrier_semaphore()
    for step in range(1, parts):
        pl.semaphore_signal(
            barrier, inc=1, device_id={"azimuth": lax.rem(me + step, parts)}, device_id_type=MESH
        )

    @pl.when(has_low)
    def _():
        pl.semaphore_signal(barrier, inc=1, device_id={"polar": band - 1}, device_id_type=MESH)

    @pl.when(has_high)
    def _():
        pl.semaphore_signal(barrier, inc=1, device_id={"polar": band + 1}, device_id_type=MESH)

    for part in range(parts):
        w_perm[part * LANES : (part + 1) * LANES, :] = w_in[
            part * chan_part : part * chan_part + LANES, :
        ]
        w_perm[parts * LANES + part * tail : parts * LANES + (part + 1) * tail, :] = w_in[
            part * chan_part + LANES : (part + 1) * chan_part, :
        ]

    neighbours = jnp.where(has_low, 1, 0) + jnp.where(has_high, 1, 0)
    pl.semaphore_wait(barrier, parts - 1 + neighbours)

    def out_copy(step, tile):
        peer = lax.rem(me + step, parts)
        return pltpu.make_async_remote_copy(
            src_ref=send.at[peer, tile], dst_ref=recv.at[tile, me],
            send_sem=a_send.at[step, tile], recv_sem=a_recv.at[step, tile],
            device_id={"azimuth": peer}, device_id_type=MESH,
        )

    def in_copy(step, tile):
        peer = lax.rem(me + parts - step, parts)
        return pltpu.make_async_remote_copy(
            src_ref=send.at[peer, tile], dst_ref=recv.at[tile, peer],
            send_sem=a_send.at[step, tile], recv_sem=a_recv.at[step, tile],
            device_id={"azimuth": peer}, device_id_type=MESH,
        )

    def row_order(it):
        return lax.rem(it * (rows - 1), rows)

    piece = 2 * LANES

    def mlp_row(it, carry):
        row = row_order(it)
        for at in range(0, hidden, piece):
            pre = dot(conv[row], w_in[:, at : at + piece]) + b_in[:, at : at + piece]
            back = dot_nt(grad[row], w_out[at : at + piece, :])
            slope[:, at : at + piece] = (back * gelu_slope(pre)).astype(BF16)
        full = dot_nt(slope[...], w_perm[...]).astype(BF16)
        for part in range(parts):
            send[part, row] = full[:, part * LANES : (part + 1) * LANES]
        tails[row] = full[:, parts * LANES :]
        recv[row, me] = send[me, row]
        for step in range(1, parts):
            out_copy(step, row).start()
        return carry

    lax.fori_loop(0, rows, mlp_row, 0)
    for part in range(parts):
        send[part, rows] = jnp.concatenate(
            [tails[row][:, part * tail : (part + 1) * tail] for row in range(rows)], axis=1
        )
    recv[rows, me] = send[me, rows]
    for step in range(1, parts):
        out_copy(step, rows).start()

    index = lax.broadcasted_iota(jnp.int32, (bases2, LANES), 0)
    half = bases2 // 2
    index = jnp.where(index >= half, index - half, index)
    source = lax.rem(index, width)
    lane_row = lax.broadcasted_iota(jnp.int32, (bases2, LANES), 1) // tail
    weights = wexp[...]
    top = weights.astype(BF16).astype(F32)
    first = lax.broadcasted_iota(jnp.int32, weights.shape, 0) < half
    weights = jnp.where(first, top, weights - top)
    w_main = weights[:, :LANES]
    w_tail = weights[:, LANES:]
    goal = target[...]
    f_t = fsel[...]

    reach2 = 2 * REACH + 1

    def pair_gain(idx, carry):
        j = idx // reach2
        shift = lax.rem(idx, reach2)
        keep = (goal == j) & (source == j + shift)
        gain[idx] = dot_tn(f_t, jnp.where(keep, w_main, 0.0).astype(BF16))
        return carry

    lax.fori_loop(0, rows * reach2, pair_gain, 0)

    def tail_gain(shift, carry):
        keep = (goal == lane_row) & (source == lane_row + shift)
        gain[rows * reach2 + shift] = dot_tn(f_t, jnp.where(keep, w_tail, 0.0).astype(BF16))
        return carry

    lax.fori_loop(0, reach2, tail_gain, 0)

    @pl.when(jnp.logical_not(has_low))
    def _():
        spec[0:REACH] = jnp.zeros((REACH, modes2, LANES), BF16)
        spec_tail[0] = jnp.zeros((modes2, LANES), BF16)

    @pl.when(jnp.logical_not(has_high))
    def _():
        spec[REACH + rows :] = jnp.zeros((REACH, modes2, LANES), BF16)
        spec_tail[2] = jnp.zeros((modes2, LANES), BF16)

    def up_copy(row):
        if row == rows:
            src, dst = spec_tail.at[1], spec_tail.at[0]
        else:
            src, dst = spec.at[REACH + row], spec.at[REACH + row - rows]
        return pltpu.make_async_remote_copy(
            src_ref=src, dst_ref=dst, send_sem=z_send.at[0, row], recv_sem=z_recv.at[0, row],
            device_id={"polar": band + 1}, device_id_type=MESH,
        )

    def down_copy(row):
        if row == rows:
            src, dst = spec_tail.at[1], spec_tail.at[2]
        else:
            src, dst = spec.at[REACH + row], spec.at[REACH + row + rows]
        return pltpu.make_async_remote_copy(
            src_ref=src, dst_ref=dst, send_sem=z_send.at[1, row], recv_sem=z_recv.at[1, row],
            device_id={"polar": band - 1}, device_id_type=MESH,
        )

    def start_up(row):
        @pl.when(has_high)
        def _():
            up_copy(row).start()

    def start_down(row):
        @pl.when(has_low)
        def _():
            down_copy(row).start()

    def analyze(tile):
        for step in range(1, parts):
            in_copy(step, tile).wait_recv()
        total = dot(ana[0], recv[tile, 0])
        for src in range(1, parts):
            total = total + dot(ana[src], recv[tile, src])
        return total.astype(BF16)

    later = []
    for it in range(rows):
        row = it * (rows - 1) % rows
        spec[REACH + row] = analyze(row)
        if row >= rows - REACH:
            if row >= rows - REACH + 1:
                start_up(row)
            else:
                later.append((start_up, row))
        if row < REACH:
            if row < REACH - 1:
                start_down(row)
            else:
                later.append((start_down, row))
    for start, row in later:
        start(row)
    spec_tail[1] = analyze(rows)
    start_up(rows)
    start_down(rows)

    def back_copy(step, tile):
        peer = lax.rem(me + step, parts)
        return pltpu.make_async_remote_copy(
            src_ref=ret_send.at[peer, tile], dst_ref=ret_recv.at[me, tile],
            send_sem=r_send.at[step, tile], recv_sem=r_recv.at[step, tile],
            device_id={"azimuth": peer}, device_id_type=MESH,
        )

    def back_in(step, tile):
        peer = lax.rem(me + parts - step, parts)
        return pltpu.make_async_remote_copy(
            src_ref=ret_send.at[peer, tile], dst_ref=ret_recv.at[peer, tile],
            send_sem=r_send.at[step, tile], recv_sem=r_recv.at[step, tile],
            device_id={"azimuth": peer}, device_id_type=MESH,
        )

    chunk = 64

    def finish(tile):
        values = outspec[...]
        for part in range(parts):
            ret_send[part, tile] = dot(syn[part], values).astype(BF16)
        ret_recv[me, tile] = ret_send[me, tile]
        for step in range(1, parts):
            back_copy(step, tile).start()

    def filter_main(j):
        def one(it, carry):
            lo = pl.ds(it * chunk, chunk)
            hi = pl.ds(modes + it * chunk, chunk)
            real = jnp.zeros((chunk, LANES), F32)
            imag = jnp.zeros((chunk, LANES), F32)
            for shift in range(reach2):
                gr, gi = gain[j * reach2 + shift, lo, :], gain[j * reach2 + shift, hi, :]
                sr = spec[j + shift, lo, :].astype(F32)
                si = spec[j + shift, hi, :].astype(F32)
                real = real + gr * sr + gi * si
                imag = imag + gr * si - gi * sr
            outspec[lo, :] = real.astype(BF16)
            outspec[hi, :] = imag.astype(BF16)
            return carry

        lax.fori_loop(0, modes // chunk, one, 0)

    def window(ref, at, shift):
        low, own, high = (ref[k, at, :].astype(F32) for k in range(3))
        result = []
        lane = lax.broadcasted_iota(jnp.int32, own.shape, 1)
        delta = (shift - REACH) * tail
        if delta == 0:
            return own
        if delta < 0:
            turn = -delta
            return jnp.where(lane < turn, pltpu.roll(low, turn, 1), pltpu.roll(own, turn, 1))
        turn = LANES - delta
        return jnp.where(lane < turn, pltpu.roll(own, turn, 1), pltpu.roll(high, turn, 1))

    def filter_tail():
        def one(it, carry):
            lo = pl.ds(it * chunk, chunk)
            hi = pl.ds(modes + it * chunk, chunk)
            real = jnp.zeros((chunk, LANES), F32)
            imag = jnp.zeros((chunk, LANES), F32)
            for shift in range(reach2):
                at = rows * reach2 + shift
                gr, gi = gain[at, lo, :], gain[at, hi, :]
                sr, si = window(spec_tail, lo, shift), window(spec_tail, hi, shift)
                real = real + gr * sr + gi * si
                imag = imag + gr * si - gi * sr
            outspec[lo, :] = real.astype(BF16)
            outspec[hi, :] = imag.astype(BF16)
            return carry

        lax.fori_loop(0, modes // chunk, one, 0)

    low_left = list(range(rows - REACH, rows))
    high_left = list(range(REACH))

    def wait_low(row):
        if row in low_left:
            low_left.remove(row)

            @pl.when(has_low)
            def _():
                up_copy(row).wait_recv()

    def wait_high(row):
        if row in high_left:
            high_left.remove(row)

            @pl.when(has_high)
            def _():
                down_copy(row).wait_recv()

    for j in sorted(range(rows), key=lambda j: max(REACH - j, j + REACH - rows + 1)):
        for row in range(j - REACH, 0):
            wait_low(row + rows)
        for row in range(rows, j + REACH + 1):
            wait_high(row - rows)
        filter_main(j)
        finish(j)

    @pl.when(has_low)
    def _():
        up_copy(rows).wait_recv()

    @pl.when(has_high)
    def _():
        down_copy(rows).wait_recv()

    filter_tail()
    finish(rows)

    for tile in range(rows + 1):
        for step in range(1, parts):
            out_copy(step, tile).wait_send()
    for row in list(range(rows - REACH, rows)) + [rows]:

        @pl.when(has_high)
        def _():
            up_copy(row).wait_send()

    for row in list(range(REACH)) + [rows]:

        @pl.when(has_low)
        def _():
            down_copy(row).wait_send()

    for tile in range(rows + 1):
        for step in range(1, parts):
            back_in(step, tile).wait_recv()
    for row in range(rows):
        pieces = []
        for src in range(parts):
            pieces.append(ret_recv[src, row])
            pieces.append(ret_recv[src, rows][:, row * tail : (row + 1) * tail])
        out[row] = jnp.concatenate(pieces, axis=1)
    for tile in range(rows + 1):
        for step in range(1, parts):
            back_copy(step, tile).wait_send()


def on_device(parts, bands, conv_out, grad_out, w_in, b_in, w_out, basis_weight, filt, offsets):
    rows, lon, channels = conv_out.shape
    hidden = w_in.shape[1]
    chan_part = channels // parts
    tail = chan_part - LANES
    assert 0 < tail and rows * tail == LANES and rows >= REACH
    modes2 = filt.shape[2]
    modes = modes2 // 2
    bases = filt.shape[0]
    width = rows + 2 * REACH
    analysis, synth = fourier_tables(parts * lon, modes)
    ana = np.ascontiguousarray(
        analysis.reshape(parts, lon, modes2).transpose(0, 2, 1)
    ).astype(ml_dtypes.bfloat16)
    syn = synth.reshape(parts, lon, modes2).astype(ml_dtypes.bfloat16)
    start_lat = lax.axis_index("polar") * rows
    start_chan = lax.axis_index("azimuth") * chan_part
    pad = ((0, 0), (REACH, REACH), (0, 0))
    fsel = lax.dynamic_slice_in_dim(jnp.pad(filt, pad), start_lat, width, 1)
    fsel = fsel.reshape(bases * width, modes2)
    fsel = jnp.concatenate([fsel, fsel], axis=0)
    goal = lax.dynamic_slice_in_dim(jnp.pad(offsets.T, pad[:2]), start_lat, width, 1) - start_lat
    goal = goal.reshape(bases * width)
    goal = jnp.broadcast_to(jnp.concatenate([goal, goal])[:, None], (2 * bases * width, LANES))
    weights = lax.dynamic_slice_in_dim(basis_weight, start_chan, chan_part, 1)
    wexp = jnp.concatenate([weights[:, :LANES]] + [weights[:, LANES:]] * rows, axis=1)
    wexp = jnp.broadcast_to(wexp[None, :, None, :], (2, bases, width, 2 * LANES))
    wexp = wexp.reshape(2 * bases * width, 2 * LANES)
    tiles = rows + 1
    vmem = pl.BlockSpec(memory_space=pltpu.VMEM)
    dma = pltpu.SemaphoreType.DMA
    reach2 = 2 * REACH + 1
    returned = pl.pallas_call(
        functools.partial(kernel, parts, bands),
        out_shape=jax.ShapeDtypeStruct((rows, lon, channels), BF16),
        in_specs=[vmem] * 10,
        out_specs=vmem,
        scratch_shapes=[
            pltpu.VMEM((channels, hidden), BF16),
            pltpu.VMEM((lon, hidden), BF16),
            pltpu.VMEM((rows, lon, parts * tail), BF16),
            pltpu.VMEM((parts, tiles, lon, LANES), BF16),
            pltpu.VMEM((tiles, parts, lon, LANES), BF16),
            pltpu.VMEM((width, modes2, LANES), BF16),
            pltpu.VMEM((3, modes2, LANES), BF16),
            pltpu.VMEM((tiles * reach2, modes2, LANES), F32),
            pltpu.VMEM((modes2, LANES), BF16),
            pltpu.VMEM((parts, tiles, lon, LANES), BF16),
            pltpu.VMEM((parts, tiles, lon, LANES), BF16),
            dma((parts, tiles)),
            dma((parts, tiles)),
            dma((2, tiles)),
            dma((2, tiles)),
            dma((parts, tiles)),
            dma((parts, tiles)),
        ],
        compiler_params=pltpu.CompilerParams(
            collective_id=0, has_side_effects=True, vmem_limit_bytes=56 * 1024 * 1024
        ),
    )(conv_out, grad_out, w_in, b_in[None, :], w_out, wexp, goal, fsel, jnp.asarray(ana),
      jnp.asarray(syn))
    return (grad_out.astype(F32) + returned.astype(F32)).astype(BF16)


def solution(mesh):
    grid = P(("member", "polar"), "azimuth", None)
    return jax.shard_map(
        functools.partial(on_device, mesh.shape["azimuth"], mesh.shape["polar"]),
        mesh=mesh,
        in_specs=(grid, grid, P(), P(), P(), P(), P(), P()),
        out_specs=grid,
        check_vma=False,
    )
```

```python
import functools
import math

import jax
import jax.numpy as jnp
import ml_dtypes
import numpy as np
from jax import lax
from jax.experimental import pallas as pl
from jax.experimental.pallas import tpu as pltpu
from jax.sharding import PartitionSpec as P

REACH = 3
LANES = 128
MESH = pl.DeviceIdType.MESH
F32 = jnp.float32
BF16 = jnp.bfloat16


def fourier_tables(length, modes):
    phase = np.arange(length)[:, None] * np.arange(modes)[None, :] % length
    angle = 2.0 * math.pi / length * phase
    scale = 1.0 / math.sqrt(length)
    factor = np.where(np.arange(modes) == 0, 1.0, 2.0)[None, :]
    analysis = np.concatenate([np.cos(angle), -np.sin(angle)], axis=1) * scale
    synth = np.concatenate([np.cos(angle) * factor, -np.sin(angle) * factor], axis=1) * scale
    return analysis, synth


def gelu_slope(values):
    normal_cdf = 0.5 * (1.0 + lax.erf(values * (1.0 / math.sqrt(2.0))))
    density = jnp.exp(-0.5 * values * values) * (1.0 / math.sqrt(2.0 * math.pi))
    return normal_cdf + values * density


def dot(a, b):
    return jnp.dot(a, b, preferred_element_type=F32)


def dot_nt(a, b):
    return lax.dot_general(a, b, (((1,), (1,)), ((), ())), preferred_element_type=F32)


def dot_tn(a, b):
    return lax.dot_general(a, b, (((0,), (0,)), ((), ())), preferred_element_type=F32)


def kernel(
    parts, bands, conv, grad, w_in, b_in, w_out, weight, filt, offsets, ana, syn,
    out,
    w_perm, slope, tails, send, recv, spec, spec_tail, gain, flipped, outspec, ret_send, ret_recv,
    a_send, a_recv, z_send, z_recv, r_send, r_recv,
):
    rows, lon, channels = conv.shape
    hidden = w_in.shape[1]
    chan_part = channels // parts
    tail = chan_part - LANES
    me = lax.axis_index("azimuth")
    band = lax.axis_index("polar")
    bases, lat, modes2 = filt.shape
    width = rows + 2 * REACH
    modes = modes2 // 2
    reach2 = 2 * REACH + 1
    has_low = band > 0
    has_high = band < bands - 1

    barrier = pltpu.get_barrier_semaphore()
    for step in range(1, parts):
        pl.semaphore_signal(
            barrier, inc=1, device_id={"azimuth": lax.rem(me + step, parts)}, device_id_type=MESH
        )

    @pl.when(has_low)
    def _():
        pl.semaphore_signal(barrier, inc=1, device_id={"polar": band - 1}, device_id_type=MESH)

    @pl.when(has_high)
    def _():
        pl.semaphore_signal(barrier, inc=1, device_id={"polar": band + 1}, device_id_type=MESH)

    for part in range(parts):
        w_perm[part * LANES : (part + 1) * LANES, :] = w_in[
            part * chan_part : part * chan_part + LANES, :
        ]
        w_perm[parts * LANES + part * tail : parts * LANES + (part + 1) * tail, :] = w_in[
            part * chan_part + LANES : (part + 1) * chan_part, :
        ]

    neighbours = jnp.where(has_low, 1, 0) + jnp.where(has_high, 1, 0)
    pl.semaphore_wait(barrier, parts - 1 + neighbours)

    def out_copy(step, tile):
        peer = lax.rem(me + step, parts)
        return pltpu.make_async_remote_copy(
            src_ref=send.at[peer, tile], dst_ref=recv.at[tile, me],
            send_sem=a_send.at[step, tile], recv_sem=a_recv.at[step, tile],
            device_id={"azimuth": peer}, device_id_type=MESH,
        )

    def in_copy(step, tile):
        peer = lax.rem(me + parts - step, parts)
        return pltpu.make_async_remote_copy(
            src_ref=send.at[peer, tile], dst_ref=recv.at[tile, peer],
            send_sem=a_send.at[step, tile], recv_sem=a_recv.at[step, tile],
            device_id={"azimuth": peer}, device_id_type=MESH,
        )

    def row_order(it):
        return lax.rem(it * (rows - 1), rows)

    piece = 2 * LANES

    def mlp_row(it, carry):
        row = row_order(it)
        for at in range(0, hidden, piece):
            pre = dot(conv[row], w_in[:, at : at + piece]) + b_in[at : at + piece][None, :]
            back = dot_nt(grad[row], w_out[at : at + piece, :])
            slope[:, at : at + piece] = (back * gelu_slope(pre)).astype(BF16)
        full = dot_nt(slope[...], w_perm[...]).astype(BF16)
        for part in range(parts):
            send[part, row] = full[:, part * LANES : (part + 1) * LANES]
        tails[row] = full[:, parts * LANES :]
        recv[row, me] = send[me, row]
        for step in range(1, parts):
            out_copy(step, row).start()
        return carry

    lax.fori_loop(0, rows, mlp_row, 0)
    for part in range(parts):
        send[part, rows] = jnp.concatenate(
            [tails[row][:, part * tail : (part + 1) * tail] for row in range(rows)], axis=1
        )
    recv[rows, me] = send[me, rows]
    for step in range(1, parts):
        out_copy(step, rows).start()

    @pl.when(jnp.logical_not(has_low))
    def _():
        spec[0:REACH] = jnp.zeros((REACH, modes2, LANES), BF16)
        spec_tail[0] = jnp.zeros((modes2, LANES), BF16)

    @pl.when(jnp.logical_not(has_high))
    def _():
        spec[REACH + rows :] = jnp.zeros((REACH, modes2, LANES), BF16)
        spec_tail[2] = jnp.zeros((modes2, LANES), BF16)

    def up_copy(row):
        if row == rows:
            src, dst = spec_tail.at[1], spec_tail.at[0]
        else:
            src, dst = spec.at[REACH + row], spec.at[REACH + row - rows]
        return pltpu.make_async_remote_copy(
            src_ref=src, dst_ref=dst, send_sem=z_send.at[0, row], recv_sem=z_recv.at[0, row],
            device_id={"polar": band + 1}, device_id_type=MESH,
        )

    def down_copy(row):
        if row == rows:
            src, dst = spec_tail.at[1], spec_tail.at[2]
        else:
            src, dst = spec.at[REACH + row], spec.at[REACH + row + rows]
        return pltpu.make_async_remote_copy(
            src_ref=src, dst_ref=dst, send_sem=z_send.at[1, row], recv_sem=z_recv.at[1, row],
            device_id={"polar": band - 1}, device_id_type=MESH,
        )

    def start_up(row):
        @pl.when(has_high)
        def _():
            up_copy(row).start()

    def start_down(row):
        @pl.when(has_low)
        def _():
            down_copy(row).start()

    def analyze(tile):
        for step in range(1, parts):
            in_copy(step, tile).wait_recv()
        total = dot(ana[0], recv[tile, 0])
        for src in range(1, parts):
            total = total + dot(ana[src], recv[tile, src])
        return total.astype(BF16)

    order = [it * (rows - 1) % rows for it in range(rows)]
    done = []
    ups = list(range(rows - 1, rows - REACH, -1))
    downs = list(range(REACH - 1))
    for row in order:
        spec[REACH + row] = analyze(row)
        done.append(row)
        while ups and ups[0] in done:
            start_up(ups.pop(0))
        while downs and downs[0] in done:
            start_down(downs.pop(0))
    spec_tail[1] = analyze(rows)
    start_up(rows)
    start_down(rows)
    start_up(rows - REACH)
    start_down(REACH - 1)

    half = bases * width
    lines = 2 * half

    def line_parts(lanes):
        line = lax.broadcasted_iota(jnp.int32, (lines, lanes), 0)
        low_bits = line >= half
        line = jnp.where(low_bits, line - half, line)
        basis = line // width
        return low_bits, basis, line - basis * width, lax.broadcasted_iota(jnp.int32, (lines, lanes), 1)

    start_lat = band * rows - REACH
    low_bits, basis, place, lane = line_parts(bases * lat)
    pick = jnp.where(lane == basis * lat + place + start_lat, 1.0, 0.0)
    pick = jnp.where((place + start_lat >= 0) & (place + start_lat < lat), pick, 0.0)
    f_t = dot(pick.astype(BF16), filt[...].reshape(bases * lat, modes2))
    low_bits, basis, place, lane = line_parts(lat)
    pick = jnp.where(lane == place + start_lat, 1.0, 0.0).astype(BF16)
    rows_of = dot(pick, offsets[...].astype(F32).astype(BF16))
    low_bits, basis, place, lane = line_parts(bases)
    goal = jnp.sum(jnp.where(lane == basis, rows_of, 0.0), axis=1, keepdims=True)
    goal = jnp.broadcast_to(goal.astype(jnp.int32) - band * rows, (lines, LANES))
    weights = weight[:, :chan_part]
    for part in range(1, parts):
        mine = weight[:, part * chan_part : (part + 1) * chan_part]
        weights = jnp.where(me == part, mine, weights)
    top = weights.astype(BF16)
    rest = (weights - top.astype(F32)).astype(BF16)
    chosen = jnp.where(lane == basis, 1.0, 0.0)
    weights = dot(jnp.where(low_bits, 0.0, chosen).astype(BF16), top) + dot(
        jnp.where(low_bits, chosen, 0.0).astype(BF16), rest
    )
    w_main = weights[:, :LANES]
    w_tail = jnp.concatenate([weights[:, LANES:]] * rows, axis=1)
    low_bits, basis, source, lane = line_parts(LANES)
    lane_row = lane // tail

    flipped[...] = jnp.transpose(f_t).astype(BF16)

    def tile_gain(tile, carry):
        goal_row = jnp.where(tile == rows, lane_row, tile)
        scale = jnp.where(tile == rows, w_tail, w_main)
        aimed = jnp.where(goal == goal_row, scale, 0.0)
        table = jnp.concatenate(
            [
                jnp.where(source == goal_row + shift, aimed, 0.0).astype(BF16)
                for shift in range(reach2)
            ],
            axis=1,
        )
        made = dot(flipped[...], table)
        for shift in range(reach2):
            gain[tile * reach2 + shift] = made[:, shift * LANES : (shift + 1) * LANES]
        return carry

    lax.fori_loop(0, rows + 1, tile_gain, 0)

    def back_copy(step, tile):
        peer = lax.rem(me + step, parts)
        return pltpu.make_async_remote_copy(
            src_ref=ret_send.at[peer, tile], dst_ref=ret_recv.at[me, tile],
            send_sem=r_send.at[step, tile], recv_sem=r_recv.at[step, tile],
            device_id={"azimuth": peer}, device_id_type=MESH,
        )

    def back_in(step, tile):
        peer = lax.rem(me + parts - step, parts)
        return pltpu.make_async_remote_copy(
            src_ref=ret_send.at[peer, tile], dst_ref=ret_recv.at[peer, tile],
            send_sem=r_send.at[step, tile], recv_sem=r_recv.at[step, tile],
            device_id={"azimuth": peer}, device_id_type=MESH,
        )

    chunk = 64

    def finish(tile):
        values = outspec[...]
        for part in range(parts):
            ret_send[part, tile] = dot(syn[part], values).astype(BF16)
        ret_recv[me, tile] = ret_send[me, tile]
        for step in range(1, parts):
            back_copy(step, tile).start()

    def filter_main(j):
        def one(it, carry):
            lo = pl.ds(it * chunk, chunk)
            hi = pl.ds(modes + it * chunk, chunk)
            real = jnp.zeros((chunk, LANES), F32)
            imag = jnp.zeros((chunk, LANES), F32)
            for shift in range(reach2):
                gr, gi = gain[j * reach2 + shift, lo, :], gain[j * reach2 + shift, hi, :]
                sr = spec[j + shift, lo, :].astype(F32)
                si = spec[j + shift, hi, :].astype(F32)
                real = real + gr * sr + gi * si
                imag = imag + gr * si - gi * sr
            outspec[lo, :] = real.astype(BF16)
            outspec[hi, :] = imag.astype(BF16)
            return carry

        lax.fori_loop(0, modes // chunk, one, 0)

    def window(ref, at, shift):
        low, own, high = (ref[k, at, :].astype(F32) for k in range(3))
        result = []
        lane = lax.broadcasted_iota(jnp.int32, own.shape, 1)
        delta = (shift - REACH) * tail
        if delta == 0:
            return own
        if delta < 0:
            turn = -delta
            return jnp.where(lane < turn, pltpu.roll(low, turn, 1), pltpu.roll(own, turn, 1))
        turn = LANES - delta
        return jnp.where(lane < turn, pltpu.roll(own, turn, 1), pltpu.roll(high, turn, 1))

    def filter_tail():
        def one(it, carry):
            lo = pl.ds(it * chunk, chunk)
            hi = pl.ds(modes + it * chunk, chunk)
            real = jnp.zeros((chunk, LANES), F32)
            imag = jnp.zeros((chunk, LANES), F32)
            for shift in range(reach2):
                at = rows * reach2 + shift
                gr, gi = gain[at, lo, :], gain[at, hi, :]
                sr, si = window(spec_tail, lo, shift), window(spec_tail, hi, shift)
                real = real + gr * sr + gi * si
                imag = imag + gr * si - gi * sr
            outspec[lo, :] = real.astype(BF16)
            outspec[hi, :] = imag.astype(BF16)
            return carry

        lax.fori_loop(0, modes // chunk, one, 0)

    low_left = list(range(rows - REACH, rows))
    high_left = list(range(REACH))

    def wait_low(row):
        if row in low_left:
            low_left.remove(row)

            @pl.when(has_low)
            def _():
                up_copy(row).wait_recv()

    def wait_high(row):
        if row in high_left:
            high_left.remove(row)

            @pl.when(has_high)
            def _():
                down_copy(row).wait_recv()

    def need_all(j):
        return j - REACH <= -REACH or j + REACH >= rows + REACH - 1

    def finish_row(j):
        for row in range(j - REACH, 0):
            wait_low(row + rows)
        for row in range(rows, j + REACH + 1):
            wait_high(row - rows)
        filter_main(j)
        finish(j)

    for j in range(rows):
        if not need_all(j):
            finish_row(j)

    @pl.when(has_low)
    def _():
        up_copy(rows).wait_recv()

    @pl.when(has_high)
    def _():
        down_copy(rows).wait_recv()

    filter_tail()
    finish(rows)
    for j in range(rows):
        if need_all(j):
            finish_row(j)

    for tile in range(rows + 1):
        for step in range(1, parts):
            out_copy(step, tile).wait_send()
    for row in list(range(rows - REACH, rows)) + [rows]:

        @pl.when(has_high)
        def _():
            up_copy(row).wait_send()

    for row in list(range(REACH)) + [rows]:

        @pl.when(has_low)
        def _():
            down_copy(row).wait_send()

    for tile in range(rows + 1):
        for step in range(1, parts):
            back_in(step, tile).wait_recv()
    for row in range(rows):
        pieces = []
        for src in range(parts):
            pieces.append(ret_recv[src, row])
            pieces.append(ret_recv[src, rows][:, row * tail : (row + 1) * tail])
        out[row] = jnp.concatenate(pieces, axis=1)
    for tile in range(rows + 1):
        for step in range(1, parts):
            back_copy(step, tile).wait_send()


def on_device(parts, bands, conv_out, grad_out, w_in, b_in, w_out, basis_weight, filt, offsets):
    rows, lon, channels = conv_out.shape
    hidden = w_in.shape[1]
    chan_part = channels // parts
    tail = chan_part - LANES
    assert 0 < tail and rows * tail == LANES and rows >= REACH
    modes2 = filt.shape[2]
    modes = modes2 // 2
    bases, width = filt.shape[0], rows + 2 * REACH
    assert filt.shape[1] <= 256
    analysis, synth = fourier_tables(parts * lon, modes)
    ana = np.ascontiguousarray(
        analysis.reshape(parts, lon, modes2).transpose(0, 2, 1)
    ).astype(ml_dtypes.bfloat16)
    syn = synth.reshape(parts, lon, modes2).astype(ml_dtypes.bfloat16)
    tiles = rows + 1
    vmem = pl.BlockSpec(memory_space=pltpu.VMEM)
    dma = pltpu.SemaphoreType.DMA
    reach2 = 2 * REACH + 1
    returned = pl.pallas_call(
        functools.partial(kernel, parts, bands),
        out_shape=jax.ShapeDtypeStruct((rows, lon, channels), BF16),
        in_specs=[vmem] * 10,
        out_specs=vmem,
        scratch_shapes=[
            pltpu.VMEM((channels, hidden), BF16),
            pltpu.VMEM((lon, hidden), BF16),
            pltpu.VMEM((rows, lon, parts * tail), BF16),
            pltpu.VMEM((parts, tiles, lon, LANES), BF16),
            pltpu.VMEM((tiles, parts, lon, LANES), BF16),
            pltpu.VMEM((width, modes2, LANES), BF16),
            pltpu.VMEM((3, modes2, LANES), BF16),
            pltpu.VMEM((tiles * reach2, modes2, LANES), F32),
            pltpu.VMEM((modes2, 2 * bases * width), BF16),
            pltpu.VMEM((modes2, LANES), BF16),
            pltpu.VMEM((parts, tiles, lon, LANES), BF16),
            pltpu.VMEM((parts, tiles, lon, LANES), BF16),
            dma((parts, tiles)),
            dma((parts, tiles)),
            dma((2, tiles)),
            dma((2, tiles)),
            dma((parts, tiles)),
            dma((parts, tiles)),
        ],
        compiler_params=pltpu.CompilerParams(
            collective_id=0, has_side_effects=True, vmem_limit_bytes=56 * 1024 * 1024
        ),
    )(conv_out, grad_out, w_in, b_in, w_out, basis_weight, filt, offsets,
      jnp.asarray(ana), jnp.asarray(syn))
    return (grad_out.astype(F32) + returned.astype(F32)).astype(BF16)


def solution(mesh):
    grid = P(("member", "polar"), "azimuth", None)
    return jax.shard_map(
        functools.partial(on_device, mesh.shape["azimuth"], mesh.shape["polar"]),
        mesh=mesh,
        in_specs=(grid, grid, P(), P(), P(), P(), P(), P()),
        out_specs=grid,
        check_vma=False,
    )
```

```python
import functools
import math

import jax
import jax.numpy as jnp
import ml_dtypes
import numpy as np
from jax import lax
from jax.experimental import pallas as pl
from jax.experimental.pallas import tpu as pltpu
from jax.sharding import PartitionSpec as P

REACH = 3
LANES = 128
MESH = pl.DeviceIdType.MESH
F32 = jnp.float32
BF16 = jnp.bfloat16


def fourier_tables(length, modes):
    phase = np.arange(length)[:, None] * np.arange(modes)[None, :] % length
    angle = 2.0 * math.pi / length * phase
    scale = 1.0 / math.sqrt(length)
    factor = np.where(np.arange(modes) == 0, 1.0, 2.0)[None, :]
    analysis = np.concatenate([np.cos(angle), -np.sin(angle)], axis=1) * scale
    synth = np.concatenate([np.cos(angle) * factor, -np.sin(angle) * factor], axis=1) * scale
    return analysis, synth


def gelu_slope(values):
    normal_cdf = 0.5 * (1.0 + lax.erf(values * (1.0 / math.sqrt(2.0))))
    density = jnp.exp(-0.5 * values * values) * (1.0 / math.sqrt(2.0 * math.pi))
    return normal_cdf + values * density


def dot(a, b):
    return jnp.dot(a, b, preferred_element_type=F32)


def dot_nt(a, b):
    return lax.dot_general(a, b, (((1,), (1,)), ((), ())), preferred_element_type=F32)


def dot_tn(a, b):
    return lax.dot_general(a, b, (((0,), (0,)), ((), ())), preferred_element_type=F32)


def kernel(
    parts, bands, conv_at, grad_at, w_in_at, b_in, w_out_at, weight, filt, offsets, ana_at, syn_at,
    out,
    conv_n, grad_n, conv, grad, w_in, w_out, ana, syn, w_perm, slope, tails, send, recv, spec, spec_tail, gain, flipped, outspec, ret_send, ret_recv,
    a_send, a_recv, z_send, z_recv, r_send, r_recv, loads,
):
    rows, lon, channels = conv.shape
    hidden = w_in.shape[1]
    chan_part = channels // parts
    tail = chan_part - LANES
    me = lax.axis_index("azimuth")
    band = lax.axis_index("polar")
    bases, lat, modes2 = filt.shape
    width = rows + 2 * REACH
    modes = modes2 // 2
    reach2 = 2 * REACH + 1
    has_low = band > 0
    has_high = band < bands - 1

    barrier = pltpu.get_barrier_semaphore()
    for step in range(1, parts):
        pl.semaphore_signal(
            barrier, inc=1, device_id={"azimuth": lax.rem(me + step, parts)}, device_id_type=MESH
        )

    @pl.when(has_low)
    def _():
        pl.semaphore_signal(barrier, inc=1, device_id={"polar": band - 1}, device_id_type=MESH)

    @pl.when(has_high)
    def _():
        pl.semaphore_signal(barrier, inc=1, device_id={"polar": band + 1}, device_id_type=MESH)

    pairs = [(conv_at, conv_n), (w_in_at, w_in), (grad_at, grad_n), (w_out_at, w_out)]
    for part in range(parts):
        split = part * chan_part + LANES
        pairs.append((w_in_at.at[part * chan_part : split], w_perm.at[part * LANES : (part + 1) * LANES]))
        begin = parts * LANES + part * tail
        pairs.append((w_in_at.at[split : split + tail], w_perm.at[begin : begin + tail]))
    pairs += [(ana_at, ana), (syn_at, syn)]
    copies = [pltpu.make_async_copy(src, dst, loads.at[n]) for n, (src, dst) in enumerate(pairs)]
    for copy in copies:
        copy.start()
    copies[0].wait()
    conv[...] = jnp.transpose(conv_n[...], (1, 0, 2))
    copies[2].wait()
    grad[...] = jnp.transpose(grad_n[...], (1, 0, 2))
    for copy in [copies[1]] + copies[3:-1]:
        copy.wait()
    neighbours = jnp.where(has_low, 1, 0) + jnp.where(has_high, 1, 0)
    pl.semaphore_wait(barrier, parts - 1 + neighbours)

    def out_copy(step, tile):
        peer = lax.rem(me + step, parts)
        return pltpu.make_async_remote_copy(
            src_ref=send.at[peer, tile], dst_ref=recv.at[tile, me],
            send_sem=a_send.at[step, tile], recv_sem=a_recv.at[step, tile],
            device_id={"azimuth": peer}, device_id_type=MESH,
        )

    def in_copy(step, tile):
        peer = lax.rem(me + parts - step, parts)
        return pltpu.make_async_remote_copy(
            src_ref=send.at[peer, tile], dst_ref=recv.at[tile, peer],
            send_sem=a_send.at[step, tile], recv_sem=a_recv.at[step, tile],
            device_id={"azimuth": peer}, device_id_type=MESH,
        )

    def row_order(it):
        return lax.rem(it * (rows - 1), rows)

    piece = 2 * LANES

    def mlp_row(row):
        for at in range(0, hidden, piece):
            pre = dot(conv[row], w_in[:, at : at + piece]) + b_in[at : at + piece][None, :]
            back = dot_nt(grad[row], w_out[at : at + piece, :])
            slope[:, at : at + piece] = (back * gelu_slope(pre)).astype(BF16)
        full = dot_nt(slope[...], w_perm[...]).astype(BF16)
        for part in range(parts):
            send[part, row] = full[:, part * LANES : (part + 1) * LANES]
        tails[row] = full[:, parts * LANES :]
        recv[row, me] = send[me, row]
        for step in range(1, parts):
            out_copy(step, row).start()

    @pl.when(jnp.logical_not(has_low))
    def _():
        spec[0:REACH] = jnp.zeros((REACH, modes2, LANES), BF16)
        spec_tail[0] = jnp.zeros((modes2, LANES), BF16)

    @pl.when(jnp.logical_not(has_high))
    def _():
        spec[REACH + rows :] = jnp.zeros((REACH, modes2, LANES), BF16)
        spec_tail[2] = jnp.zeros((modes2, LANES), BF16)

    def up_copy(row):
        if isinstance(row, int) and row == rows:
            src, dst = spec_tail.at[1], spec_tail.at[0]
        else:
            src, dst = spec.at[REACH + row], spec.at[REACH + row - rows]
        return pltpu.make_async_remote_copy(
            src_ref=src, dst_ref=dst, send_sem=z_send.at[0, row], recv_sem=z_recv.at[0, row],
            device_id={"polar": band + 1}, device_id_type=MESH,
        )

    def down_copy(row):
        if isinstance(row, int) and row == rows:
            src, dst = spec_tail.at[1], spec_tail.at[2]
        else:
            src, dst = spec.at[REACH + row], spec.at[REACH + row + rows]
        return pltpu.make_async_remote_copy(
            src_ref=src, dst_ref=dst, send_sem=z_send.at[1, row], recv_sem=z_recv.at[1, row],
            device_id={"polar": band - 1}, device_id_type=MESH,
        )

    def start_up(row):
        @pl.when(has_high)
        def _():
            up_copy(row).start()

    def start_down(row):
        @pl.when(has_low)
        def _():
            down_copy(row).start()

    def analyze(tile):
        for step in range(1, parts):
            in_copy(step, tile).wait_recv()
        total = dot(ana[0], recv[tile, 0])
        for src in range(1, parts):
            total = total + dot(ana[src], recv[tile, src])
        return total.astype(BF16)

    delay = 2

    def advance(it, carry):
        @pl.when(it < rows)
        def _():
            mlp_row(row_order(it))

        @pl.when(it == rows - 1)
        def _():
            for part in range(parts):
                send[part, rows] = jnp.concatenate(
                    [tails[row][:, part * tail : (part + 1) * tail] for row in range(rows)], axis=1
                )
            recv[rows, me] = send[me, rows]
            for step in range(1, parts):
                out_copy(step, rows).start()

        @pl.when(it >= delay)
        def _():
            row = row_order(it - delay)
            spec[REACH + row] = analyze(row)

            @pl.when(has_high & (row >= rows - REACH))
            def _():
                up_copy(row).start()

            @pl.when(has_low & (row == 0))
            def _():
                down_copy(row).start()

        return carry

    lax.fori_loop(0, rows + delay, advance, 0)
    for row in range(1, REACH):
        start_down(row)
    spec_tail[1] = analyze(rows)
    start_up(rows)
    start_down(rows)

    half = bases * width
    lines = 2 * half

    def line_parts(lanes):
        line = lax.broadcasted_iota(jnp.int32, (lines, lanes), 0)
        low_bits = line >= half
        line = jnp.where(low_bits, line - half, line)
        basis = line // width
        return low_bits, basis, line - basis * width, lax.broadcasted_iota(jnp.int32, (lines, lanes), 1)

    start_lat = band * rows - REACH
    low_bits, basis, place, lane = line_parts(bases * lat)
    pick = jnp.where(lane == basis * lat + place + start_lat, 1.0, 0.0)
    pick = jnp.where((place + start_lat >= 0) & (place + start_lat < lat), pick, 0.0)
    f_t = dot(pick.astype(BF16), filt[...].reshape(bases * lat, modes2))
    low_bits, basis, place, lane = line_parts(lat)
    pick = jnp.where(lane == place + start_lat, 1.0, 0.0).astype(BF16)
    rows_of = dot(pick, offsets[...].astype(F32).astype(BF16))
    low_bits, basis, place, lane = line_parts(bases)
    goal = jnp.sum(jnp.where(lane == basis, rows_of, 0.0), axis=1, keepdims=True)
    goal = jnp.broadcast_to(goal.astype(jnp.int32) - band * rows, (lines, LANES))
    weights = weight[:, :chan_part]
    for part in range(1, parts):
        mine = weight[:, part * chan_part : (part + 1) * chan_part]
        weights = jnp.where(me == part, mine, weights)
    top = weights.astype(BF16)
    rest = (weights - top.astype(F32)).astype(BF16)
    chosen = jnp.where(lane == basis, 1.0, 0.0)
    weights = dot(jnp.where(low_bits, 0.0, chosen).astype(BF16), top) + dot(
        jnp.where(low_bits, chosen, 0.0).astype(BF16), rest
    )
    w_main = weights[:, :LANES]
    w_tail = jnp.concatenate([weights[:, LANES:]] * rows, axis=1)
    low_bits, basis, source, lane = line_parts(LANES)
    lane_row = lane // tail

    flipped[...] = jnp.transpose(f_t).astype(BF16)

    def tile_gain(tile, carry):
        goal_row = jnp.where(tile == rows, lane_row, tile)
        scale = jnp.where(tile == rows, w_tail, w_main)
        aimed = jnp.where(goal == goal_row, scale, 0.0)
        table = jnp.concatenate(
            [
                jnp.where(source == goal_row + shift, aimed, 0.0).astype(BF16)
                for shift in range(reach2)
            ],
            axis=1,
        )
        made = dot(flipped[...], table)
        for shift in range(reach2):
            gain[tile * reach2 + shift] = made[:, shift * LANES : (shift + 1) * LANES]
        return carry

    lax.fori_loop(0, rows + 1, tile_gain, 0)

    def back_copy(step, tile):
        peer = lax.rem(me + step, parts)
        return pltpu.make_async_remote_copy(
            src_ref=ret_send.at[peer, tile], dst_ref=ret_recv.at[me, tile],
            send_sem=r_send.at[step, tile], recv_sem=r_recv.at[step, tile],
            device_id={"azimuth": peer}, device_id_type=MESH,
        )

    def back_in(step, tile):
        peer = lax.rem(me + parts - step, parts)
        return pltpu.make_async_remote_copy(
            src_ref=ret_send.at[peer, tile], dst_ref=ret_recv.at[peer, tile],
            send_sem=r_send.at[step, tile], recv_sem=r_recv.at[step, tile],
            device_id={"azimuth": peer}, device_id_type=MESH,
        )

    chunk = 64

    def finish(tile):
        values = outspec[...]
        for part in range(parts):
            ret_send[part, tile] = dot(syn[part], values).astype(BF16)
        ret_recv[me, tile] = ret_send[me, tile]
        for step in range(1, parts):
            back_copy(step, tile).start()

    def filter_main(j):
        def one(it, carry):
            lo = pl.ds(it * chunk, chunk)
            hi = pl.ds(modes + it * chunk, chunk)
            real = jnp.zeros((chunk, LANES), F32)
            imag = jnp.zeros((chunk, LANES), F32)
            for shift in range(reach2):
                gr, gi = gain[j * reach2 + shift, lo, :], gain[j * reach2 + shift, hi, :]
                sr = spec[j + shift, lo, :].astype(F32)
                si = spec[j + shift, hi, :].astype(F32)
                real = real + gr * sr + gi * si
                imag = imag + gr * si - gi * sr
            outspec[lo, :] = real.astype(BF16)
            outspec[hi, :] = imag.astype(BF16)
            return carry

        lax.fori_loop(0, modes // chunk, one, 0)

    def window(ref, at, shift):
        low, own, high = (ref[k, at, :].astype(F32) for k in range(3))
        result = []
        lane = lax.broadcasted_iota(jnp.int32, own.shape, 1)
        delta = (shift - REACH) * tail
        if delta == 0:
            return own
        if delta < 0:
            turn = -delta
            return jnp.where(lane < turn, pltpu.roll(low, turn, 1), pltpu.roll(own, turn, 1))
        turn = LANES - delta
        return jnp.where(lane < turn, pltpu.roll(own, turn, 1), pltpu.roll(high, turn, 1))

    def filter_tail():
        def one(it, carry):
            lo = pl.ds(it * chunk, chunk)
            hi = pl.ds(modes + it * chunk, chunk)
            real = jnp.zeros((chunk, LANES), F32)
            imag = jnp.zeros((chunk, LANES), F32)
            for shift in range(reach2):
                at = rows * reach2 + shift
                gr, gi = gain[at, lo, :], gain[at, hi, :]
                sr, si = window(spec_tail, lo, shift), window(spec_tail, hi, shift)
                real = real + gr * sr + gi * si
                imag = imag + gr * si - gi * sr
            outspec[lo, :] = real.astype(BF16)
            outspec[hi, :] = imag.astype(BF16)
            return carry

        lax.fori_loop(0, modes // chunk, one, 0)

    copies[-1].wait()
    low_left = list(range(rows - REACH, rows))
    high_left = list(range(REACH))

    def wait_low(row):
        if row in low_left:
            low_left.remove(row)

            @pl.when(has_low)
            def _():
                up_copy(row).wait_recv()

    def wait_high(row):
        if row in high_left:
            high_left.remove(row)

            @pl.when(has_high)
            def _():
                down_copy(row).wait_recv()

    def need_all(j):
        return j - REACH <= -REACH or j + REACH >= rows + REACH - 1

    def finish_row(j):
        for row in range(j - REACH, 0):
            wait_low(row + rows)
        for row in range(rows, j + REACH + 1):
            wait_high(row - rows)
        filter_main(j)
        finish(j)

    for j in sorted(range(rows), key=need_all):
        finish_row(j)

    @pl.when(has_low)
    def _():
        up_copy(rows).wait_recv()

    @pl.when(has_high)
    def _():
        down_copy(rows).wait_recv()

    filter_tail()
    finish(rows)

    for tile in range(rows + 1):
        for step in range(1, parts):
            out_copy(step, tile).wait_send()
    for row in list(range(rows - REACH, rows)) + [rows]:

        @pl.when(has_high)
        def _():
            up_copy(row).wait_send()

    for row in list(range(REACH)) + [rows]:

        @pl.when(has_low)
        def _():
            down_copy(row).wait_send()

    for tile in range(rows + 1):
        for step in range(1, parts):
            back_in(step, tile).wait_recv()
    for row in range(rows):
        pieces = []
        for src in range(parts):
            pieces.append(ret_recv[src, row])
            pieces.append(ret_recv[src, rows][:, row * tail : (row + 1) * tail])
        conv[row] = jnp.concatenate(pieces, axis=1)
    out[...] = jnp.transpose(conv[...], (1, 0, 2))
    for tile in range(rows + 1):
        for step in range(1, parts):
            back_copy(step, tile).wait_send()


def on_device(parts, bands, conv_out, grad_out, w_in, b_in, w_out, basis_weight, filt, offsets):
    rows, lon, channels = conv_out.shape
    hidden = w_in.shape[1]
    chan_part = channels // parts
    tail = chan_part - LANES
    assert 0 < tail and rows * tail == LANES and rows >= REACH
    modes2 = filt.shape[2]
    modes = modes2 // 2
    bases, width = filt.shape[0], rows + 2 * REACH
    assert filt.shape[1] <= 256
    analysis, synth = fourier_tables(parts * lon, modes)
    ana = np.ascontiguousarray(
        analysis.reshape(parts, lon, modes2).transpose(0, 2, 1)
    ).astype(ml_dtypes.bfloat16)
    syn = synth.reshape(parts, lon, modes2).astype(ml_dtypes.bfloat16)
    tiles = rows + 1
    vmem = pl.BlockSpec(memory_space=pltpu.VMEM)
    hbm = pl.BlockSpec(memory_space=pl.ANY)
    dma = pltpu.SemaphoreType.DMA
    reach2 = 2 * REACH + 1
    returned = pl.pallas_call(
        functools.partial(kernel, parts, bands),
        out_shape=jax.ShapeDtypeStruct((lon, rows, channels), BF16),
        in_specs=[hbm, hbm, hbm, vmem, hbm, vmem, vmem, vmem, hbm, hbm],
        out_specs=vmem,
        scratch_shapes=[
            pltpu.VMEM((lon, rows, channels), BF16),
            pltpu.VMEM((lon, rows, channels), BF16),
            pltpu.VMEM((rows, lon, channels), BF16),
            pltpu.VMEM((rows, lon, channels), BF16),
            pltpu.VMEM(w_in.shape, BF16),
            pltpu.VMEM(w_out.shape, BF16),
            pltpu.VMEM(ana.shape, BF16),
            pltpu.VMEM(syn.shape, BF16),
            pltpu.VMEM((channels, hidden), BF16),
            pltpu.VMEM((lon, hidden), BF16),
            pltpu.VMEM((rows, lon, parts * tail), BF16),
            pltpu.VMEM((parts, tiles, lon, LANES), BF16),
            pltpu.VMEM((tiles, parts, lon, LANES), BF16),
            pltpu.VMEM((width, modes2, LANES), BF16),
            pltpu.VMEM((3, modes2, LANES), BF16),
            pltpu.VMEM((tiles * reach2, modes2, LANES), F32),
            pltpu.VMEM((modes2, 2 * bases * width), BF16),
            pltpu.VMEM((modes2, LANES), BF16),
            pltpu.VMEM((parts, tiles, lon, LANES), BF16),
            pltpu.VMEM((parts, tiles, lon, LANES), BF16),
            dma((parts, tiles)),
            dma((parts, tiles)),
            dma((2, tiles)),
            dma((2, tiles)),
            dma((parts, tiles)),
            dma((parts, tiles)),
            dma((6 + 2 * parts,)),
        ],
        compiler_params=pltpu.CompilerParams(
            collective_id=0, has_side_effects=True, vmem_limit_bytes=56 * 1024 * 1024
        ),
    )(jnp.transpose(conv_out, (1, 0, 2)), jnp.transpose(grad_out, (1, 0, 2)), w_in, b_in, w_out, basis_weight, filt, offsets,
      jnp.asarray(ana), jnp.asarray(syn))
    return (grad_out.astype(F32) + jnp.transpose(returned, (1, 0, 2)).astype(F32)).astype(BF16)


def solution(mesh):
    grid = P(("member", "polar"), "azimuth", None)
    return jax.shard_map(
        functools.partial(on_device, mesh.shape["azimuth"], mesh.shape["polar"]),
        mesh=mesh,
        in_specs=(grid, grid, P(), P(), P(), P(), P(), P()),
        out_specs=grid,
        check_vma=False,
    )
```

```python
import functools
import math

import jax
import jax.numpy as jnp
import ml_dtypes
import numpy as np
from jax import lax
from jax.experimental import pallas as pl
from jax.experimental.pallas import tpu as pltpu
from jax.sharding import PartitionSpec as P

REACH = 3
LANES = 128
MESH = pl.DeviceIdType.MESH
F32 = jnp.float32
BF16 = jnp.bfloat16


def fourier_tables(length, modes):
    phase = np.arange(length)[:, None] * np.arange(modes)[None, :] % length
    angle = 2.0 * math.pi / length * phase
    scale = 1.0 / math.sqrt(length)
    factor = np.where(np.arange(modes) == 0, 1.0, 2.0)[None, :]
    analysis = np.concatenate([np.cos(angle), -np.sin(angle)], axis=1) * scale
    synth = np.concatenate([np.cos(angle) * factor, -np.sin(angle) * factor], axis=1) * scale
    return analysis, synth


def gelu_slope(values):
    normal_cdf = 0.5 * (1.0 + lax.erf(values * (1.0 / math.sqrt(2.0))))
    density = jnp.exp(-0.5 * values * values) * (1.0 / math.sqrt(2.0 * math.pi))
    return normal_cdf + values * density


def dot(a, b):
    return jnp.dot(a, b, preferred_element_type=F32)


def dot_nt(a, b):
    return lax.dot_general(a, b, (((1,), (1,)), ((), ())), preferred_element_type=F32)


def dot_tn(a, b):
    return lax.dot_general(a, b, (((0,), (0,)), ((), ())), preferred_element_type=F32)


def kernel(
    parts, bands, conv_at, grad_at, w_in_at, b_in, w_out_at, weight, filt, offsets, ana_at, syn_at,
    out,
    conv_n, grad_n, conv, grad, w_in, w_out, ana, syn, w_perm, slope, tails, send, recv, spec, spec_tail, gain, flipped, outspec, ret_send, ret_recv,
    a_send, a_recv, z_send, z_recv, r_send, r_recv, loads,
):
    rows, lon, channels = conv.shape
    hidden = w_in.shape[1]
    chan_part = channels // parts
    tail = chan_part - LANES
    me = lax.axis_index("azimuth")
    band = lax.axis_index("polar")
    bases, lat, modes2 = filt.shape
    width = rows + 2 * REACH
    modes = modes2 // 2
    reach2 = 2 * REACH + 1
    has_low = band > 0
    has_high = band < bands - 1

    barrier = pltpu.get_barrier_semaphore()
    for step in range(1, parts):
        pl.semaphore_signal(
            barrier, inc=1, device_id={"azimuth": lax.rem(me + step, parts)}, device_id_type=MESH
        )

    @pl.when(has_low)
    def _():
        pl.semaphore_signal(barrier, inc=1, device_id={"polar": band - 1}, device_id_type=MESH)

    @pl.when(has_high)
    def _():
        pl.semaphore_signal(barrier, inc=1, device_id={"polar": band + 1}, device_id_type=MESH)

    pairs = [(conv_at, conv_n), (w_in_at, w_in), (grad_at, grad_n), (w_out_at, w_out)]
    for part in range(parts):
        split = part * chan_part + LANES
        pairs.append((w_in_at.at[part * chan_part : split], w_perm.at[part * LANES : (part + 1) * LANES]))
        begin = parts * LANES + part * tail
        pairs.append((w_in_at.at[split : split + tail], w_perm.at[begin : begin + tail]))
    pairs += [(ana_at, ana), (syn_at, syn)]
    copies = [pltpu.make_async_copy(src, dst, loads.at[n]) for n, (src, dst) in enumerate(pairs)]
    for copy in copies:
        copy.start()
    copies[0].wait()
    conv[...] = jnp.transpose(conv_n[...], (1, 0, 2))
    copies[2].wait()
    grad[...] = jnp.transpose(grad_n[...], (1, 0, 2))
    for copy in [copies[1]] + copies[3:-1]:
        copy.wait()
    neighbours = jnp.where(has_low, 1, 0) + jnp.where(has_high, 1, 0)
    pl.semaphore_wait(barrier, parts - 1 + neighbours)

    def out_copy(step, tile):
        peer = lax.rem(me + step, parts)
        return pltpu.make_async_remote_copy(
            src_ref=send.at[peer, tile], dst_ref=recv.at[tile, me],
            send_sem=a_send.at[step, tile], recv_sem=a_recv.at[step, tile],
            device_id={"azimuth": peer}, device_id_type=MESH,
        )

    def in_copy(step, tile):
        peer = lax.rem(me + parts - step, parts)
        return pltpu.make_async_remote_copy(
            src_ref=send.at[peer, tile], dst_ref=recv.at[tile, peer],
            send_sem=a_send.at[step, tile], recv_sem=a_recv.at[step, tile],
            device_id={"azimuth": peer}, device_id_type=MESH,
        )

    def row_order(it):
        return lax.rem(it * (rows - 1), rows)

    piece = 2 * LANES

    def mlp_row(row):
        for at in range(0, hidden, piece):
            pre = dot(conv[row], w_in[:, at : at + piece]) + b_in[at : at + piece][None, :]
            back = dot_nt(grad[row], w_out[at : at + piece, :])
            slope[:, at : at + piece] = (back * gelu_slope(pre)).astype(BF16)
        full = dot_nt(slope[...], w_perm[...]).astype(BF16)
        for part in range(parts):
            send[part, row] = full[:, part * LANES : (part + 1) * LANES]
        tails[row] = full[:, parts * LANES :]
        recv[row, me] = send[me, row]
        for step in range(1, parts):
            out_copy(step, row).start()

    @pl.when(jnp.logical_not(has_low))
    def _():
        spec[0:REACH] = jnp.zeros((REACH, modes2, LANES), BF16)
        spec_tail[0] = jnp.zeros((modes2, LANES), BF16)

    @pl.when(jnp.logical_not(has_high))
    def _():
        spec[REACH + rows :] = jnp.zeros((REACH, modes2, LANES), BF16)
        spec_tail[2] = jnp.zeros((modes2, LANES), BF16)

    def up_copy(row):
        if isinstance(row, int) and row == rows:
            src, dst = spec_tail.at[1], spec_tail.at[0]
        else:
            src, dst = spec.at[REACH + row], spec.at[REACH + row - rows]
        return pltpu.make_async_remote_copy(
            src_ref=src, dst_ref=dst, send_sem=z_send.at[0, row], recv_sem=z_recv.at[0, row],
            device_id={"polar": band + 1}, device_id_type=MESH,
        )

    def down_copy(row):
        if isinstance(row, int) and row == rows:
            src, dst = spec_tail.at[1], spec_tail.at[2]
        else:
            src, dst = spec.at[REACH + row], spec.at[REACH + row + rows]
        return pltpu.make_async_remote_copy(
            src_ref=src, dst_ref=dst, send_sem=z_send.at[1, row], recv_sem=z_recv.at[1, row],
            device_id={"polar": band - 1}, device_id_type=MESH,
        )

    def start_up(row):
        @pl.when(has_high)
        def _():
            up_copy(row).start()

    def start_down(row):
        @pl.when(has_low)
        def _():
            down_copy(row).start()

    def analyze(tile):
        for step in range(1, parts):
            in_copy(step, tile).wait_recv()
        total = dot(ana[0], recv[tile, 0])
        for src in range(1, parts):
            total = total + dot(ana[src], recv[tile, src])
        return total.astype(BF16)

    delay = 2

    def advance(it, carry):
        @pl.when(it < rows)
        def _():
            mlp_row(row_order(it))

        @pl.when(it == rows - 1)
        def _():
            for part in range(parts):
                send[part, rows] = jnp.concatenate(
                    [tails[row][:, part * tail : (part + 1) * tail] for row in range(rows)], axis=1
                )
            recv[rows, me] = send[me, rows]
            for step in range(1, parts):
                out_copy(step, rows).start()

        @pl.when(it >= delay)
        def _():
            row = row_order(it - delay)
            spec[REACH + row] = analyze(row)

            @pl.when(has_high & (row >= rows - REACH))
            def _():
                up_copy(row).start()

            @pl.when(has_low & (row == 0))
            def _():
                down_copy(row).start()

        return carry

    lax.fori_loop(0, rows + delay, advance, 0)
    for row in range(1, REACH):
        start_down(row)
    spec_tail[1] = analyze(rows)
    start_up(rows)
    start_down(rows)

    half = bases * width
    lines = 2 * half

    def line_parts(lanes):
        line = lax.broadcasted_iota(jnp.int32, (lines, lanes), 0)
        low_bits = line >= half
        line = jnp.where(low_bits, line - half, line)
        basis = line // width
        return low_bits, basis, line - basis * width, lax.broadcasted_iota(jnp.int32, (lines, lanes), 1)

    start_lat = band * rows - REACH
    low_bits, basis, place, lane = line_parts(bases * lat)
    pick = jnp.where(lane == basis * lat + place + start_lat, 1.0, 0.0)
    pick = jnp.where((place + start_lat >= 0) & (place + start_lat < lat), pick, 0.0)
    f_t = dot(pick.astype(BF16), filt[...].reshape(bases * lat, modes2))
    low_bits, basis, place, lane = line_parts(lat)
    pick = jnp.where(lane == place + start_lat, 1.0, 0.0).astype(BF16)
    rows_of = dot(pick, offsets[...].astype(F32).astype(BF16))
    low_bits, basis, place, lane = line_parts(bases)
    goal = jnp.sum(jnp.where(lane == basis, rows_of, 0.0), axis=1, keepdims=True)
    goal = jnp.broadcast_to(goal.astype(jnp.int32) - band * rows, (lines, LANES))
    weights = weight[:, :chan_part]
    for part in range(1, parts):
        mine = weight[:, part * chan_part : (part + 1) * chan_part]
        weights = jnp.where(me == part, mine, weights)
    top = weights.astype(BF16)
    rest = (weights - top.astype(F32)).astype(BF16)
    chosen = jnp.where(lane == basis, 1.0, 0.0)
    weights = dot(jnp.where(low_bits, 0.0, chosen).astype(BF16), top) + dot(
        jnp.where(low_bits, chosen, 0.0).astype(BF16), rest
    )
    w_main = weights[:, :LANES]
    w_tail = jnp.concatenate([weights[:, LANES:]] * rows, axis=1)
    low_bits, basis, source, lane = line_parts(LANES)
    lane_row = lane // tail

    flipped[...] = jnp.transpose(f_t).astype(BF16)

    def tile_gain(tile, carry):
        goal_row = jnp.where(tile == rows, lane_row, tile)
        scale = jnp.where(tile == rows, w_tail, w_main)
        aimed = jnp.where(goal == goal_row, scale, 0.0)
        table = jnp.concatenate(
            [
                jnp.where(source == goal_row + shift, aimed, 0.0).astype(BF16)
                for shift in range(reach2)
            ],
            axis=1,
        )
        made = dot(flipped[...], table)
        for shift in range(reach2):
            gain[tile * reach2 + shift] = made[:, shift * LANES : (shift + 1) * LANES]
        return carry

    lax.fori_loop(0, rows + 1, tile_gain, 0)

    def back_copy(step, tile):
        peer = lax.rem(me + step, parts)
        return pltpu.make_async_remote_copy(
            src_ref=ret_send.at[peer, tile], dst_ref=ret_recv.at[me, tile],
            send_sem=r_send.at[step, tile], recv_sem=r_recv.at[step, tile],
            device_id={"azimuth": peer}, device_id_type=MESH,
        )

    def back_in(step, tile):
        peer = lax.rem(me + parts - step, parts)
        return pltpu.make_async_remote_copy(
            src_ref=ret_send.at[peer, tile], dst_ref=ret_recv.at[peer, tile],
            send_sem=r_send.at[step, tile], recv_sem=r_recv.at[step, tile],
            device_id={"azimuth": peer}, device_id_type=MESH,
        )

    chunk = 64

    def finish(tile):
        values = outspec[...]
        for part in range(parts):
            ret_send[part, tile] = dot(syn[part], values).astype(BF16)
        ret_recv[me, tile] = ret_send[me, tile]
        for step in range(1, parts):
            back_copy(step, tile).start()

    def filter_main(j):
        def one(it, carry):
            lo = pl.ds(it * chunk, chunk)
            hi = pl.ds(modes + it * chunk, chunk)
            real = jnp.zeros((chunk, LANES), F32)
            imag = jnp.zeros((chunk, LANES), F32)
            for shift in range(reach2):
                gr, gi = gain[j * reach2 + shift, lo, :], gain[j * reach2 + shift, hi, :]
                sr = spec[j + shift, lo, :].astype(F32)
                si = spec[j + shift, hi, :].astype(F32)
                real = real + gr * sr + gi * si
                imag = imag + gr * si - gi * sr
            outspec[lo, :] = real.astype(BF16)
            outspec[hi, :] = imag.astype(BF16)
            return carry

        lax.fori_loop(0, modes // chunk, one, 0)

    def window(ref, at, shift):
        low, own, high = (ref[k, at, :].astype(F32) for k in range(3))
        result = []
        lane = lax.broadcasted_iota(jnp.int32, own.shape, 1)
        delta = (shift - REACH) * tail
        if delta == 0:
            return own
        if delta < 0:
            turn = -delta
            return jnp.where(lane < turn, pltpu.roll(low, turn, 1), pltpu.roll(own, turn, 1))
        turn = LANES - delta
        return jnp.where(lane < turn, pltpu.roll(own, turn, 1), pltpu.roll(high, turn, 1))

    def filter_tail():
        def one(it, carry):
            lo = pl.ds(it * chunk, chunk)
            hi = pl.ds(modes + it * chunk, chunk)
            real = jnp.zeros((chunk, LANES), F32)
            imag = jnp.zeros((chunk, LANES), F32)
            for shift in range(reach2):
                at = rows * reach2 + shift
                gr, gi = gain[at, lo, :], gain[at, hi, :]
                sr, si = window(spec_tail, lo, shift), window(spec_tail, hi, shift)
                real = real + gr * sr + gi * si
                imag = imag + gr * si - gi * sr
            outspec[lo, :] = real.astype(BF16)
            outspec[hi, :] = imag.astype(BF16)
            return carry

        lax.fori_loop(0, modes // chunk, one, 0)

    copies[-1].wait()
    low_left = list(range(rows - REACH, rows))
    high_left = list(range(REACH))

    def wait_low(row):
        if row in low_left:
            low_left.remove(row)

            @pl.when(has_low)
            def _():
                up_copy(row).wait_recv()

    def wait_high(row):
        if row in high_left:
            high_left.remove(row)

            @pl.when(has_high)
            def _():
                down_copy(row).wait_recv()

    def need_all(j):
        return j - REACH <= -REACH or j + REACH >= rows + REACH - 1

    def finish_row(j):
        for row in range(j - REACH, 0):
            wait_low(row + rows)
        for row in range(rows, j + REACH + 1):
            wait_high(row - rows)
        filter_main(j)
        finish(j)

    for j in sorted(range(rows), key=need_all):
        finish_row(j)

    @pl.when(has_low)
    def _():
        up_copy(rows).wait_recv()

    @pl.when(has_high)
    def _():
        down_copy(rows).wait_recv()

    filter_tail()
    finish(rows)

    for tile in range(rows + 1):
        for step in range(1, parts):
            out_copy(step, tile).wait_send()
    for row in list(range(rows - REACH, rows)) + [rows]:

        @pl.when(has_high)
        def _():
            up_copy(row).wait_send()

    for row in list(range(REACH)) + [rows]:

        @pl.when(has_low)
        def _():
            down_copy(row).wait_send()

    for tile in range(rows + 1):
        for step in range(1, parts):
            back_in(step, tile).wait_recv()
    for row in range(rows):
        pieces = []
        for src in range(parts):
            pieces.append(ret_recv[src, row])
            pieces.append(ret_recv[src, rows][:, row * tail : (row + 1) * tail])
        total = grad[row].astype(F32) + jnp.concatenate(pieces, axis=1).astype(F32)
        conv[row] = total.astype(BF16)
    out[...] = jnp.transpose(conv[...], (1, 0, 2))
    for tile in range(rows + 1):
        for step in range(1, parts):
            back_copy(step, tile).wait_send()


def on_device(parts, bands, conv_out, grad_out, w_in, b_in, w_out, basis_weight, filt, offsets):
    rows, lon, channels = conv_out.shape
    hidden = w_in.shape[1]
    chan_part = channels // parts
    tail = chan_part - LANES
    assert 0 < tail and rows * tail == LANES and rows >= REACH
    modes2 = filt.shape[2]
    modes = modes2 // 2
    bases, width = filt.shape[0], rows + 2 * REACH
    assert filt.shape[1] <= 256
    analysis, synth = fourier_tables(parts * lon, modes)
    ana = np.ascontiguousarray(
        analysis.reshape(parts, lon, modes2).transpose(0, 2, 1)
    ).astype(ml_dtypes.bfloat16)
    syn = synth.reshape(parts, lon, modes2).astype(ml_dtypes.bfloat16)
    tiles = rows + 1
    vmem = pl.BlockSpec(memory_space=pltpu.VMEM)
    hbm = pl.BlockSpec(memory_space=pl.ANY)
    dma = pltpu.SemaphoreType.DMA
    reach2 = 2 * REACH + 1
    result = pl.pallas_call(
        functools.partial(kernel, parts, bands),
        out_shape=jax.ShapeDtypeStruct((lon, rows, channels), BF16),
        in_specs=[hbm, hbm, hbm, vmem, hbm, vmem, vmem, vmem, hbm, hbm],
        out_specs=vmem,
        scratch_shapes=[
            pltpu.VMEM((lon, rows, channels), BF16),
            pltpu.VMEM((lon, rows, channels), BF16),
            pltpu.VMEM((rows, lon, channels), BF16),
            pltpu.VMEM((rows, lon, channels), BF16),
            pltpu.VMEM(w_in.shape, BF16),
            pltpu.VMEM(w_out.shape, BF16),
            pltpu.VMEM(ana.shape, BF16),
            pltpu.VMEM(syn.shape, BF16),
            pltpu.VMEM((channels, hidden), BF16),
            pltpu.VMEM((lon, hidden), BF16),
            pltpu.VMEM((rows, lon, parts * tail), BF16),
            pltpu.VMEM((parts, tiles, lon, LANES), BF16),
            pltpu.VMEM((tiles, parts, lon, LANES), BF16),
            pltpu.VMEM((width, modes2, LANES), BF16),
            pltpu.VMEM((3, modes2, LANES), BF16),
            pltpu.VMEM((tiles * reach2, modes2, LANES), F32),
            pltpu.VMEM((modes2, 2 * bases * width), BF16),
            pltpu.VMEM((modes2, LANES), BF16),
            pltpu.VMEM((parts, tiles, lon, LANES), BF16),
            pltpu.VMEM((parts, tiles, lon, LANES), BF16),
            dma((parts, tiles)),
            dma((parts, tiles)),
            dma((2, tiles)),
            dma((2, tiles)),
            dma((parts, tiles)),
            dma((parts, tiles)),
            dma((6 + 2 * parts,)),
        ],
        compiler_params=pltpu.CompilerParams(
            collective_id=0, has_side_effects=True, vmem_limit_bytes=56 * 1024 * 1024
        ),
    )(jnp.transpose(conv_out, (1, 0, 2)), jnp.transpose(grad_out, (1, 0, 2)), w_in, b_in, w_out, basis_weight, filt, offsets,
      jnp.asarray(ana), jnp.asarray(syn))
    return jnp.transpose(result, (1, 0, 2))


def solution(mesh):
    grid = P(("member", "polar"), "azimuth", None)
    return jax.shard_map(
        functools.partial(on_device, mesh.shape["azimuth"], mesh.shape["polar"]),
        mesh=mesh,
        in_specs=(grid, grid, P(), P(), P(), P(), P(), P()),
        out_specs=grid,
        check_vma=False,
    )
```
